768 devices in a mesh: outer: 24 (over y_hi, z), inner: 8 (over x, core), head: 4 (over y_lo).
Axes of the slice: x: 4, y: 8 (y_hi: 2, y_lo: 4; y = y_hi * 4 + y_lo), z: 12, core: 2. Of those that a mesh axis runs over, the one named last changes fastest.
Arguments:
- query: bfloat16 [24576, 6144], P(('outer', 'inner'), 'head'), may hold values from -6 to 6
- key: bfloat16 [24576, 1024], P(('outer', 'inner', 'head')), may hold values from -6 to 6
- value: bfloat16 [24576, 1024], P(('outer', 'inner', 'head')), may hold values from -6 to 6
- output_cotangent: bfloat16 [24576, 6144], P(('outer', 'inner'), 'head'), may hold values from -6 to 6
- segment: int32 [24576], replicated, may hold values from 0 to 191, never falling along the last dimension, each value on 1 to 256 neighbouring positions
Outputs:
- attended: bfloat16 [24576, 6144], P(('outer', 'inner'), 'head')
- d_query: bfloat16 [24576, 6144], P(('outer', 'inner'), 'head')
- d_key: bfloat16 [24576, 1024], P(('outer', 'inner', 'head'))
- d_value: bfloat16 [24576, 1024], P(('outer', 'inner', 'head'))
The draws below stay inside these ranges and needn't reach their ends.
Inputs may be any that keep to these rules, and one draw needn't show every extreme that they name: `segment`: ids never fall along the row; every document has 1 to 256 tokens, and some document has exactly 256.
All inputs are finite; a program needn't handle non-finite values.
Results may differ from the reference program's by a relative error of at most 0.03.
Values may be sent and summed in bfloat16 or wider, within the bound.
No kernel may reach another device: no remote copies, remote signals or barrier semaphores. Data moves between devices by JAX's collectives and lax.ppermute only.
A program may use at most 32 MiB of HBM per device.

```python
import math
import jax
import jax.numpy as jnp
import numpy as np
from jax import lax

QUERY_HEADS = 48
KEY_VALUE_HEADS = 8
HEAD_SIZE = 128
CONTEXT_TOKENS = 128
REACH = 2
ROW_TOKENS = 24576
DOCS = 192


def draw_query(key, part):
    value_rows = jnp.clip(jax.random.normal(jax.random.fold_in(key, 11), (ROW_TOKENS, QUERY_HEADS * HEAD_SIZE), jnp.float32), -6.0, 6.0)
    return value_rows.astype(jnp.bfloat16)


def draw_key(key, part):
    value_rows = jnp.clip(jax.random.normal(jax.random.fold_in(key, 13), (ROW_TOKENS, KEY_VALUE_HEADS * HEAD_SIZE), jnp.float32), -6.0, 6.0)
    return value_rows.astype(jnp.bfloat16)


def block_scale(own_key, extent, pieces, low, top_value):
    def one(position, parts):
        heights = jax.random.uniform(jax.random.fold_in(jax.random.fold_in(own_key, 6), position), (parts,), jnp.float32, low / len(pieces), top_value / len(pieces))
        return jnp.repeat(jnp.exp(heights), extent[position] // parts).reshape((-1,) + (1,) * (len(extent) - position - 1))

    level = one(*pieces[0])
    for cut in pieces[1:]:
        level = level * one(*cut)
    return level


def split_up(number_of, total, most, skew):
    portions = [(1 << 20) // math.isqrt(rank ** skew) + 1 for rank in range(2, number_of + 1)]
    spare, given = total - most - (number_of - 1), [1] * (number_of - 1)
    while spare > 0:
        free = [i for i in range(number_of - 1) if given[i] < most]
        mass, remaining = sum([portions[i] for i in free]), spare
        for i in free:
            addition = min(most - given[i], max(1, remaining * portions[i] // mass), spare)
            given[i] = given[i] + addition
            spare = spare - addition
    return np.array([most] + given)


def ragged_sizes(own_key, amount, total, most, lean):
    if amount == 2:
        one = jax.random.randint(own_key, (), max(1, total - most), min(most, total - 1) + 1)
        return jnp.stack([one, total - one])
    sizes = jnp.asarray(split_up(amount, total, most, lean), jnp.int32)
    couples = (amount - 1) // 2
    giver, receiver = sizes[1:1 + 2 * couples:2], sizes[2:2 + 2 * couples:2]
    slack = jnp.minimum(giver - 1, most - receiver)
    passed = jax.random.randint(jax.random.fold_in(own_key, 1), (couples,), 0, 1 << 20) % (slack + 1)
    sizes = sizes.at[1:1 + 2 * couples:2].set(giver - passed).at[2:2 + 2 * couples:2].set(receiver + passed)
    return sizes[jax.random.permutation(jax.random.fold_in(own_key, 2), amount)]


def centred(key, shape, spread, most, split=(), held_as=jnp.bfloat16):
    factor_of = block_scale(key, shape, split, -0.22, 0.18) if split else 1.0
    entries = jax.random.normal(key, shape, jnp.float32) * spread * factor_of
    return jnp.minimum(jnp.maximum(entries, -most), most).astype(held_as)


def setup_inputs(seed: int = 0) -> dict:
    arg_keys = jax.random.split(jax.random.key(seed), 6)
    query = draw_query(jax.random.fold_in(arg_keys[5], 71), 0)
    key = draw_key(jax.random.fold_in(arg_keys[5], 71), 0)
    value = centred(arg_keys[2], (ROW_TOKENS, KEY_VALUE_HEADS * HEAD_SIZE), 1.0, 6.0, ((0, 768),))
    output_cotangent = centred(arg_keys[3], (ROW_TOKENS, QUERY_HEADS * HEAD_SIZE), 1.0, 6.0, ((0, 192), (1, 4)))
    segment = jnp.searchsorted(jnp.cumsum(ragged_sizes(arg_keys[4], DOCS, ROW_TOKENS, REACH * CONTEXT_TOKENS, 2)), jnp.arange(ROW_TOKENS), side="right").astype(jnp.int32)
    return {"query": query, "key": key, "value": value, "output_cotangent": output_cotangent, "segment": segment}


def rounded(value_rows):
    return lax.optimization_barrier(value_rows.astype(jnp.bfloat16)).astype(jnp.float32)

def reference(query, key, value, output_cotangent, segment):
    query_group_width = QUERY_HEADS // KEY_VALUE_HEADS
    factor = 1.0 / math.sqrt(HEAD_SIZE)
    slice_view = (REACH + 1) * CONTEXT_TOKENS
    pad_amount = REACH * CONTEXT_TOKENS
    padded_keys = jnp.concatenate([jnp.zeros((pad_amount, KEY_VALUE_HEADS * HEAD_SIZE), key.dtype), key], 0)
    padded_values = jnp.concatenate([jnp.zeros((pad_amount, KEY_VALUE_HEADS * HEAD_SIZE), value.dtype), value], 0)
    seg_pad = jnp.concatenate([jnp.full((pad_amount,), -1, jnp.int32), segment.astype(jnp.int32)], 0)
    block_count = ROW_TOKENS // CONTEXT_TOKENS

    def one_block(totals, block_index):
        key_gradient, value_gradient = totals
        row_beginning = (block_index * CONTEXT_TOKENS).astype(jnp.int32)
        query_tile_rows = lax.dynamic_slice_in_dim(query, row_beginning, CONTEXT_TOKENS, 0).astype(jnp.float32).reshape(CONTEXT_TOKENS, KEY_VALUE_HEADS, query_group_width, HEAD_SIZE)
        block_gradients = lax.dynamic_slice_in_dim(output_cotangent, row_beginning, CONTEXT_TOKENS, 0).astype(jnp.float32).reshape(CONTEXT_TOKENS, KEY_VALUE_HEADS, query_group_width, HEAD_SIZE)
        key_slice_view = lax.dynamic_slice_in_dim(padded_keys, row_beginning, slice_view, 0).astype(jnp.float32).reshape(slice_view, KEY_VALUE_HEADS, HEAD_SIZE)
        value_slice_view = lax.dynamic_slice_in_dim(padded_values, row_beginning, slice_view, 0).astype(jnp.float32).reshape(slice_view, KEY_VALUE_HEADS, HEAD_SIZE)
        query_seg = lax.dynamic_slice_in_dim(segment.astype(jnp.int32), row_beginning, CONTEXT_TOKENS, 0)
        key_seg = lax.dynamic_slice_in_dim(seg_pad, row_beginning, slice_view, 0)
        query_pos = row_beginning + jnp.arange(CONTEXT_TOKENS, dtype=jnp.int32)
        key_pos = row_beginning - pad_amount + jnp.arange(slice_view, dtype=jnp.int32)
        allowed = (query_seg[:, None] == key_seg[None, :]) & (key_pos[None, :] <= query_pos[:, None])
        scores = jnp.einsum('tkgd,skd->kgts', query_tile_rows, key_slice_view) * factor
        scores = jnp.where(allowed, scores, -jnp.inf)
        row_max = lax.optimization_barrier(jnp.max(scores, -1, keepdims=True))
        row_total = lax.optimization_barrier(jnp.sum(jnp.exp(scores - row_max), -1, keepdims=True))
        log_total = row_max + jnp.log(row_total)
        weights = jnp.where(allowed, jnp.exp(scores - log_total), 0.0)
        weights_low = rounded(weights)
        attended = jnp.einsum('kgts,skd->tkgd', weights_low, value_slice_view).astype(jnp.bfloat16)
        delta_row = lax.optimization_barrier(jnp.sum(block_gradients * attended.astype(jnp.float32), -1))
        d_weights = jnp.einsum('tkgd,skd->kgts', block_gradients, value_slice_view)
        d_scores = weights * (d_weights - jnp.transpose(delta_row, (1, 2, 0))[..., None])
        d_scores_low = rounded(d_scores)
        d_query = (jnp.einsum('kgts,skd->tkgd', d_scores_low, key_slice_view) * factor).astype(jnp.bfloat16)
        key_portion = jnp.einsum('kgts,tkgd->skd', d_scores_low, query_tile_rows) * factor
        value_portion = jnp.einsum('kgts,tkgd->skd', weights_low, block_gradients)
        previous_key = lax.dynamic_slice_in_dim(key_gradient, row_beginning, slice_view, 0)
        previous_value = lax.dynamic_slice_in_dim(value_gradient, row_beginning, slice_view, 0)
        key_gradient = lax.dynamic_update_slice_in_dim(key_gradient, previous_key + key_portion.reshape(slice_view, KEY_VALUE_HEADS * HEAD_SIZE), row_beginning, 0)
        value_gradient = lax.dynamic_update_slice_in_dim(value_gradient, previous_value + value_portion.reshape(slice_view, KEY_VALUE_HEADS * HEAD_SIZE), row_beginning, 0)
        return ((key_gradient, value_gradient), (attended.reshape(CONTEXT_TOKENS, QUERY_HEADS * HEAD_SIZE), d_query.reshape(CONTEXT_TOKENS, QUERY_HEADS * HEAD_SIZE)))
    empty_gradient = jnp.zeros((ROW_TOKENS + pad_amount, KEY_VALUE_HEADS * HEAD_SIZE), jnp.float32)
    (key_gradient, value_gradient), (attended, d_query) = lax.scan(one_block, (empty_gradient, empty_gradient), jnp.arange(block_count, dtype=jnp.int32))
    return (attended.reshape(ROW_TOKENS, QUERY_HEADS * HEAD_SIZE), d_query.reshape(ROW_TOKENS, QUERY_HEADS * HEAD_SIZE), key_gradient[pad_amount:].astype(jnp.bfloat16), value_gradient[pad_amount:].astype(jnp.bfloat16))
```

```python
import math

import jax
import jax.numpy as jnp
from jax import lax
from jax.experimental import pallas as pl
from jax.experimental.pallas import tpu as pltpu
from jax.sharding import PartitionSpec as P

QUERY_HEADS = 48
KEY_VALUE_HEADS = 8
HEAD_SIZE = 128
GROUP = QUERY_HEADS // KEY_VALUE_HEADS
REACH = 2
TOKENS = 128
SHARDS = ("outer", "inner")
FACTOR = 1.0 / math.sqrt(HEAD_SIZE)
LOG2E = math.log2(math.e)
FAR = -1e30


def passed_along(x, by):
    devices = lax.axis_size(SHARDS)
    pairs = [(i, i + by) for i in range(devices) if 0 <= i + by < devices]
    return lax.ppermute(x, SHARDS, pairs)


def exchanged(x):
    return lax.all_to_all(x, "head", split_axis=0, concat_axis=0, tiled=True)


def nt(a, b):
    return lax.dot_general(a, b, (((1,), (1,)), ((), ())), preferred_element_type=jnp.float32)


def nn(a, b):
    return jnp.dot(a, b, preferred_element_type=jnp.float32)


def attention(
    q_ref, g_ref, kv0_ref, kv1_ref, kv2_ref, bias_ref,
    att_ref, dq_ref, own_ref, back1_ref, back2_ref, p_ref, s_ref,
):
    upper = lax.broadcasted_iota(jnp.int32, (TOKENS, TOKENS), 0) <= lax.broadcasted_iota(
        jnp.int32, (TOKENS, TOKENS), 1
    )
    for g in range(kv0_ref.shape[-1] // HEAD_SIZE):
        columns = slice(g * HEAD_SIZE, (g + 1) * HEAD_SIZE)
        keys, values = (
            [ref[:, w, :, columns].reshape(TOKENS, HEAD_SIZE) for ref in (kv2_ref, kv1_ref, kv0_ref)]
            for w in range(2)
        )
        key_rows, value_rows = jnp.concatenate(keys, 0), jnp.concatenate(values, 0)
        key_columns = jnp.concatenate([k.T for k in keys], 1)
        value_columns = jnp.concatenate([v.T for v in values], 1)
        for j in range(GROUP):
            at = slice((g * GROUP + j) * HEAD_SIZE, (g * GROUP + j + 1) * HEAD_SIZE)
            lanes = slice(j * TOKENS, (j + 1) * TOKENS)
            scores = nt(key_rows, q_ref[:, at])
            d_weights = nt(value_rows, g_ref[:, at])
            sa = jnp.where(upper, scores[2 * TOKENS :], scores[:TOKENS]) * (FACTOR * LOG2E) + bias_ref[0]
            sb = scores[TOKENS : 2 * TOKENS] * (FACTOR * LOG2E) + bias_ref[1]
            top = jnp.max(jnp.maximum(sa, sb), 0, keepdims=True)
            pa, pb = jnp.exp2(sa - top), jnp.exp2(sb - top)
            scale = 1.0 / jnp.sum(pa + pb, 0, keepdims=True)
            pa, pb = pa * scale, pb * scale
            da = jnp.where(upper, d_weights[2 * TOKENS :], d_weights[:TOKENS])
            db = d_weights[TOKENS : 2 * TOKENS]
            delta = jnp.sum(pa * da + pb * db, 0, keepdims=True)
            ea, eb = pa * (da - delta), pb * (db - delta)
            for ref, a, b in ((p_ref, pa, pb), (s_ref, ea, eb)):
                ref[:TOKENS, lanes] = jnp.where(upper, 0.0, a).astype(jnp.bfloat16)
                ref[TOKENS : 2 * TOKENS, lanes] = b.astype(jnp.bfloat16)
                ref[2 * TOKENS :, lanes] = jnp.where(upper, a, 0.0).astype(jnp.bfloat16)
        heads = [
            slice((g * GROUP + j) * HEAD_SIZE, (g * GROUP + j + 1) * HEAD_SIZE) for j in range(GROUP)
        ]
        queries = jnp.concatenate([q_ref[:, at] for at in heads], 0)
        cotangents = jnp.concatenate([g_ref[:, at] for at in heads], 0)
        d_key = nn(s_ref[...], queries) * FACTOR
        d_value = nn(p_ref[...], cotangents)
        for ref, first in ((back2_ref, 0), (back1_ref, TOKENS), (own_ref, 2 * TOKENS)):
            for w, grad in ((0, d_key), (1, d_value)):
                part = grad[first : first + TOKENS].astype(ref.dtype)
                ref[:, w, :, columns] = part.reshape(ref.shape[0], ref.shape[2], HEAD_SIZE)
        attended = nn(value_columns, p_ref[...])
        d_query = nn(key_columns, s_ref[...]) * FACTOR
        for j, at in enumerate(heads):
            lanes = slice(j * TOKENS, (j + 1) * TOKENS)
            att_ref[:, at] = attended[:, lanes].T.astype(jnp.bfloat16)
            dq_ref[:, at] = d_query[:, lanes].T.astype(jnp.bfloat16)


def pack(k_ref, v_ref, x_ref):
    width = x_ref.shape[-1]
    for c in range(x_ref.shape[0]):
        x_ref[c, 0] = k_ref[:, c * width : (c + 1) * width]
        x_ref[c, 1] = v_ref[:, c * width : (c + 1) * width]


def finish(x_ref, dk_ref, dv_ref):
    width = x_ref.shape[-1]
    for c in range(x_ref.shape[0]):
        dk_ref[:, c * width : (c + 1) * width] = x_ref[c, 0]
        dv_ref[:, c * width : (c + 1) * width] = x_ref[c, 1]


def body(query, key, value, output_cotangent, segment):
    length = query.shape[0]
    rows, width = key.shape
    members = length // rows
    width //= members
    vmem = pl.BlockSpec(memory_space=pltpu.VMEM)
    out = jax.ShapeDtypeStruct
    packed = pl.pallas_call(
        pack,
        out_shape=out((members, 2, rows, width), key.dtype),
        in_specs=[vmem] * 2,
        out_specs=vmem,
        name="pack",
    )(key, value)
    blocks = [exchanged(packed)]
    for offset in range(1, REACH + 1):
        blocks.append(passed_along(blocks[0], offset))

    shard = lax.axis_index(SHARDS)
    segments = []
    for offset in range(REACH + 1):
        source = shard - offset
        part = lax.dynamic_slice_in_dim(segment, jnp.maximum(source, 0) * length, length, 0)
        segments.append(jnp.where(source >= 0, part, -1))
    upper = jnp.arange(length)[:, None] <= jnp.arange(length)[None, :]
    mine = segments[0][None, :]
    meets = jnp.stack(
        [
            jnp.where(upper, segments[0][:, None], segments[2][:, None]) == mine,
            segments[1][:, None] == mine,
        ]
    )
    bias = jnp.where(meets, 0.0, FAR)

    block = blocks[0].shape
    attended, d_query, own, back1, back2 = pl.pallas_call(
        attention,
        out_shape=(
            out(query.shape, query.dtype),
            out(query.shape, query.dtype),
            out(block, jnp.float32),
            out(block, jnp.bfloat16),
            out(block, jnp.bfloat16),
        ),
        in_specs=[vmem] * 6,
        out_specs=[vmem] * 5,
        scratch_shapes=[pltpu.VMEM((3 * TOKENS, GROUP * TOKENS), jnp.bfloat16)] * 2,
        compiler_params=pltpu.CompilerParams(vmem_limit_bytes=24 * 1024 * 1024),
        name="attention",
    )(query, output_cotangent, *blocks, bias)

    back = [passed_along(back1, -1), passed_along(back2, -2)]
    total = own + back[0].astype(jnp.float32) + back[1].astype(jnp.float32)
    gathered = exchanged(total.astype(jnp.bfloat16))
    d_key, d_value = pl.pallas_call(
        finish,
        out_shape=(out(key.shape, key.dtype), out(value.shape, value.dtype)),
        in_specs=[vmem],
        out_specs=[vmem] * 2,
        name="finish",
    )(gathered)
    return attended, d_query, d_key, d_value


def solution(mesh):
    in_specs = (
        P(("outer", "inner"), "head"),
        P(("outer", "inner", "head"), None),
        P(("outer", "inner", "head"), None),
        P(("outer", "inner"), "head"),
        P(),
    )
    out_specs = (
        P(("outer", "inner"), "head"),
        P(("outer", "inner"), "head"),
        P(("outer", "inner", "head"), None),
        P(("outer", "inner", "head"), None),
    )
    return jax.shard_map(body, mesh=mesh, in_specs=in_specs, out_specs=out_specs, check_vma=False)
```
